128 devices in a mesh: wide: 16 (over z_hi, x, core), narrow: 8 (over z_lo, y).
Axes of the slice: x: 4, y: 4, z: 4 (z_hi: 2, z_lo: 2; z = z_hi * 2 + z_lo), core: 2. Of those that a mesh axis runs over, the one named last changes fastest.
Arguments:
- points: float32 [8, 32768], P(None, 'narrow'), may hold values from 0 to 1
- scales: float32 [8], replicated, may hold values from 2 to 6
- frequencies: float32 [8, 32768], P(None, 'wide'), may hold values from -24 to 24
- phases: float32 [32768], P('wide'), may hold values from -3.140625 to 3.140625
- feature_weights: bfloat16 [64, 32768], P(None, 'wide'), may hold values from -6 to 6
- targets: float32 [32768], P(('narrow', 'wide')), may hold values from -6 to 6
- noise: float32 [64, 32768], P(None, ('narrow', 'wide')), may hold values from -1.8 to 1.8
- inverses: float32 [2, 8192, 8192], P(None, 'wide', 'narrow'), may hold values from -0.01767767 to 1.0176777
- groups: int32 [2, 64], replicated, may hold values from 0 to 255, as said below
Outputs:
- residual: float32 [64, 32768], P(None, ('narrow', 'wide'))
- weights: float32 [2, 64, 8192], P(None, None, 'wide')
The draws below stay inside these ranges and needn't reach their ends.
Inputs may be any that keep to these rules, and one draw needn't show every extreme that they name: All entries differ; each names the group of points g * 128 to g * 128 + 127. In every block, the entries n * 8 to (n + 1) * 8 - 1 name groups of narrow index n's points, that is groups n * 32 to (n + 1) * 32 - 1.
All inputs are finite; a program needn't handle non-finite values.
Results may differ from the reference program's by a relative error of at most 0.00065.
Values may be sent and summed in bfloat16 or wider, within the bound.
A program may use at most 128 MiB of HBM per device.

```python
import math
import jax
import jax.numpy as jnp
from jax import lax

D = 8
FEATURES = 32768
SAMPLES = 64
BLOCK = 8192
GROUP = 128
BLOCKS = 2
SHARD_PTS = 4096
POINTS = 32768
N_NARROW = 8


def draw_inverses(key, part):
    first_key, second_key = jax.random.split(jax.random.fold_in(key, 11))
    diagonal = jax.random.uniform(first_key, (BLOCKS, BLOCK), jnp.float32, 0.5, 1.0)
    offdiag = jax.random.truncated_normal(second_key, -4.0, 4.0, (BLOCKS, BLOCK, BLOCK), jnp.float32) * (0.4 / math.sqrt(BLOCK))
    positions = jnp.arange(BLOCK)
    return offdiag.at[:, positions, positions].add(diagonal)


def draw_groups(key, part):
    per_shard = SHARD_PTS // GROUP
    taken = BLOCK // (N_NARROW * GROUP)
    shard_keys = jax.random.split(jax.random.fold_in(key, 23), N_NARROW)
    orders = jax.vmap(lambda one_key: jax.random.permutation(one_key, per_shard))(shard_keys)
    chosen = orders[:, :BLOCKS * taken].astype(jnp.int32) + (jnp.arange(N_NARROW, dtype=jnp.int32) * per_shard)[:, None]
    chosen = chosen.reshape(N_NARROW, BLOCKS, taken)
    return jnp.transpose(chosen, (1, 0, 2)).reshape(BLOCKS, N_NARROW * taken).astype(jnp.int32)


def block_levels(key, extent, shards, smallest, high):
    def one(axis_at, blocks):
        draws = jax.random.uniform(jax.random.fold_in(jax.random.fold_in(key, 6), axis_at), (blocks,), jnp.float32, smallest / len(shards), high / len(shards))
        return jnp.repeat(jnp.exp(draws), extent[axis_at] // blocks).reshape((-1,) + (1,) * (len(extent) - axis_at - 1))

    level = one(*shards[0])
    for cut in shards[1:]:
        level = level * one(*cut)
    return level


def gaussian(rng, shape, scale, limit, cuts=(), kind=jnp.bfloat16):
    entries = scale * jax.random.normal(rng, shape, jnp.float32)
    if cuts:
        entries = entries * block_levels(rng, shape, cuts, -0.22, 0.18)
    return jnp.clip(entries, -limit, limit).astype(kind)


def setup_inputs(seed: int = 0) -> dict:
    key_list = jax.random.split(jax.random.key(seed), 10)
    points = jnp.clip(1.0 * jax.random.uniform(key_list[0], (D, POINTS), jnp.float32) ** block_levels(key_list[0], (D, POINTS), ((1, 8),), -0.2, 0.2), 0.0, 1.0)
    scales = jnp.clip(jnp.exp(jax.random.uniform(key_list[1], (D,), jnp.float32, math.log(2.0), math.log(6.0))), 2.0, 6.0)
    frequencies = gaussian(key_list[2], (D, FEATURES), 4.0, 24.0, ((1, 16),), jnp.float32)
    phases = jnp.clip(jax.random.uniform(key_list[3], (FEATURES,), jnp.float32, -3.140625, 3.140625), -3.140625, 3.140625)
    feature_weights = gaussian(key_list[4], (SAMPLES, FEATURES), 1.0, 6.0, ((1, 16),))
    targets = gaussian(key_list[5], (POINTS,), 1.0, 6.0, ((0, 128),), jnp.float32)
    noise = gaussian(key_list[6], (SAMPLES, POINTS), 0.3, 1.8, ((1, 128),), jnp.float32)
    inverses = draw_inverses(jax.random.fold_in(key_list[9], 71), 0)
    groups = draw_groups(jax.random.fold_in(key_list[9], 71), 0)
    return dict(points=points, scales=scales, frequencies=frequencies, phases=phases, feature_weights=feature_weights, targets=targets, noise=noise, inverses=inverses, groups=groups)


NOISE_VAR = 0.1
ROOT_FIVE = math.sqrt(5.0)
HIGH = lax.Precision.HIGHEST

def matern_tile(rows_coords, cols_coords, row_ids, col_ids):
    dist_sq = jnp.zeros((rows_coords.shape[1], cols_coords.shape[1]), rows_coords.dtype)
    for coord in range(rows_coords.shape[0]):
        differ = rows_coords[coord][:, None] - cols_coords[coord][None, :]
        dist_sq = dist_sq + differ * differ
    scaled = ROOT_FIVE * jnp.sqrt(dist_sq)
    values = (1.0 + scaled + scaled * scaled / 3.0) * jnp.exp(-scaled)
    return values + jnp.where(row_ids[:, None] == col_ids[None, :], NOISE_VAR, 0.0)

def reference(points, scales, frequencies, phases, feature_weights, targets, noise, inverses, groups):
    total_points = points.shape[1]
    pblock = math.gcd(total_points, 512)

    def prior_block(index):
        coords = lax.dynamic_slice_in_dim(points, index * pblock, pblock, 1)
        angles = jnp.dot(frequencies.T, coords, precision=HIGH, preferred_element_type=jnp.float32) + phases[:, None]
        features = jnp.cos(angles).astype(jnp.bfloat16)
        return jnp.dot(feature_weights, features, preferred_element_type=jnp.float32)
    blocks = lax.map(prior_block, jnp.arange(total_points // pblock, dtype=jnp.int32))
    prior = jnp.transpose(blocks, (1, 0, 2)).reshape(SAMPLES, total_points)
    residual = targets[None, :] - math.sqrt(2.0 / FEATURES) * prior - noise
    scaled = scales[:, None] * points
    col_ids_all = jnp.arange(total_points, dtype=jnp.int32)
    cblock = math.gcd(total_points, 2048)
    weight_list = []
    for block_index in range(BLOCKS):
        member_ids = (groups[block_index][:, None] * GROUP + jnp.arange(GROUP, dtype=jnp.int32)[None, :]).reshape(-1)
        picked = jnp.take(residual, member_ids, axis=1)
        update = jnp.dot(picked, inverses[block_index].T, precision=HIGH, preferred_element_type=jnp.float32)
        row_coords = jnp.take(scaled, member_ids, axis=1)

        def kernel_block(index):
            begin = index * cblock
            tile = matern_tile(row_coords, lax.dynamic_slice_in_dim(scaled, begin, cblock, 1), member_ids, lax.dynamic_slice_in_dim(col_ids_all, begin, cblock, 0))
            return jnp.dot(update, tile, precision=HIGH, preferred_element_type=jnp.float32)
        parts = lax.map(kernel_block, jnp.arange(total_points // cblock, dtype=jnp.int32))
        residual = residual - jnp.transpose(parts, (1, 0, 2)).reshape(SAMPLES, total_points)
        weight_list.append(update)
    return (residual, jnp.stack(weight_list))
```

```python
import math

import jax
import jax.numpy as jnp
from jax import lax
from jax.experimental import pallas as pl
from jax.experimental.pallas import tpu as pltpu
from jax.sharding import PartitionSpec as P

F32 = jnp.float32
BF16 = jnp.bfloat16
MESH = pl.DeviceIdType.MESH

D = 8
NW = 16
NN = 8
SAMPLES = 64
GROUP = 128
NGROUPS = 32
PAIRS = 16
KDIM = 64
FHERE = 2048
FCHUNK = 512
ROWS = 512
BCOLS = 1024
NOISE_VAR = 0.1
LN2 = math.log(2.0)
LOG2E = 1.0 / LN2
ROUND = 12582912.0
SIN = (6.283185005, -41.34165573, 81.60100555, -76.54978180, 39.53670502)


def split3(value):
    first = value.astype(BF16).astype(F32)
    rest = value - first
    second = rest.astype(BF16).astype(F32)
    return first, second, rest - second


def rows_of(*rows):
    at = lax.broadcasted_iota(jnp.int32, (8, GROUP), 0)
    result = jnp.zeros((8, GROUP), F32)
    for index, row in enumerate(rows):
        result = jnp.where(at == index, row, result)
    return result


def left_stack(value, extra):
    a, b, c = split3(value)
    return jnp.concatenate([a, a, b, b, a, c, extra, jnp.zeros_like(a)], axis=0)


def right_stack(value, extra):
    a, b, c = split3(value)
    return jnp.concatenate([a, b, a, b, c, a, extra, jnp.zeros_like(a)], axis=0)


def cosine_turns(turns):
    whole = (turns + ROUND) - ROUND
    s = 0.25 - jnp.abs(turns - whole)
    y = s * s
    return s * (SIN[0] + y * (SIN[1] + y * (SIN[2] + y * (SIN[3] + y * SIN[4]))))


def arrange(groups, points, ordered, row_points, place, mine):
    w = lax.axis_index("wide")
    n = lax.axis_index("narrow")

    def group_of(g):
        return points[:, pl.ds(pl.multiple_of(g * GROUP, GROUP), GROUP)]

    member = [lax.rem(groups[k // 8, n * 8 + k % 8], NGROUPS) for k in range(16)]
    for k in range(8):
        row_points[k] = group_of(lax.rem(groups[k // 4, w * 4 + k % 4], NGROUPS))

    @pl.loop(0, NGROUPS)
    def _(g):
        below = jnp.int32(0)
        hits = jnp.int32(0)
        spot = jnp.int32(0)
        for k in range(16):
            below = below + jnp.where(member[k] < g, 1, 0)
            hit = member[k] == g
            hits = hits + jnp.where(hit, 1, 0)
            spot = spot + jnp.where(hit, k, 0)
        at = jnp.where(hits > 0, spot, 16 + g - below)
        place[g] = at
        ordered[at] = group_of(g)
        for i in range(2):
            mine[i, at] = jnp.where(g == 2 * w + i, 1.0, 0.0)


def body(
    place, mine, scales, points, row_points, freq, phases, fw, targets, noise, inverses,
    out, weights,
    amat, bmat, cmat, armat, rows, base, q, h_hi, h_lo, inv_v, inv_hi, inv_lo,
    rs_buf, r_buf, r_hl, wp, nb, wf, w_hl, own, give, cbuf, ubuf, xbuf, vbuf, zbuf,
    inv_sem, wsend, wrecv, nsend, nrecv, rsend, rrecv, fsend, frecv,
):
    w = lax.axis_index("wide")
    n = lax.axis_index("narrow")
    core = lax.rem(w, 2)
    x_here = lax.rem(lax.div(w, 2), 4)
    z_here = lax.div(w, 8)

    def wide_dev(peer):
        return {"wide": peer}

    def narrow_dev(peer):
        return {"narrow": peer}

    barrier = pltpu.get_barrier_semaphore()

    @pl.loop(1, NW)
    def _(d):
        pl.semaphore_signal(barrier, inc=1, device_id=wide_dev(lax.rem(w + d, NW)), device_id_type=MESH)

    @pl.loop(1, NN)
    def _(d):
        pl.semaphore_signal(barrier, inc=1, device_id=narrow_dev(lax.rem(n + d, NN)), device_id_type=MESH)

    inv_copy = pltpu.make_async_copy(inverses, inv_v, inv_sem)
    inv_copy.start()

    scale_col = jnp.concatenate([jnp.full((1, GROUP), scales[d], F32) for d in range(D)], axis=0)
    coord_scale = scale_col * (math.sqrt(5.0) * LOG2E)
    ones = jnp.ones((1, GROUP), F32)

    @pl.loop(0, FHERE // GROUP)
    def _(k):
        at = pl.ds(pl.multiple_of(k * GROUP, GROUP), GROUP)
        f = freq[:, at] * (0.5 / math.pi)
        ph = split3(phases[:, at] * (0.5 / math.pi))
        amat[at, :] = left_stack(f, rows_of(*ph)).T.astype(BF16)

    @pl.loop(0, NGROUPS)
    def _(g):
        pts = points[g]
        bmat[g] = right_stack(pts, rows_of(ones, ones, ones)).astype(BF16)
        z = (pts - 0.5) * coord_scale
        t = split3(jnp.sum(z * z, axis=0, keepdims=True))
        cmat[g] = right_stack(z, rows_of(ones, ones, ones, *t)).astype(BF16)

    for i in range(2):
        at = slice(i * GROUP, (i + 1) * GROUP)
        base[i] = targets[:, at] - noise[:, at]

    def prior_pairs(lo, hi):
        @pl.loop(lo, hi)
        def _(pair):
            rhs = jnp.concatenate([bmat[2 * pair], bmat[2 * pair + 1]], axis=1)
            acc = jnp.zeros((SAMPLES, 2 * GROUP), F32)
            for k in range(FHERE // FCHUNK):
                at = slice(k * FCHUNK, (k + 1) * FCHUNK)
                turns = jnp.dot(amat[at, :], rhs, preferred_element_type=F32)
                features = cosine_turns(turns).astype(BF16)
                acc = acc + jnp.dot(fw[:, at], features, preferred_element_type=F32)
            for i in range(2):
                at = 2 * pair + i
                own_base = mine[0, at] * base[0] + mine[1, at] * base[1]
                q[at] = own_base - acc[:, i * GROUP : (i + 1) * GROUP] * (1.0 / 128.0)

    def kernel_pairs(lo, hi):
        @pl.loop(lo, hi)
        def _(pair):
            rhs = jnp.concatenate([cmat[2 * pair], cmat[2 * pair + 1]], axis=1)
            for b in range(2):
                for k in range(2):
                    at = slice(k * 256, (k + 1) * 256)
                    m = jnp.dot(armat[b, at, :], rhs, preferred_element_type=F32)
                    m = jnp.maximum(m, 1e-12)
                    u = m * lax.rsqrt(m)
                    h = (1.0 + u * LN2 + m * (LN2 * LN2 / 3.0)) * jnp.exp2(-u)
                    hi_part = h.astype(BF16)
                    h_hi[b, pair, at, :] = hi_part
                    h_lo[b, pair, at, :] = (h - hi_part.astype(F32)).astype(BF16)

    def wide_chunk(ref, peer):
        return ref.at[lax.div(peer, 2), pl.ds(pl.multiple_of(lax.rem(peer, 2) * 32, 32), 32)]

    def wide_copy(b, phase, d, gather):
        peer = lax.rem(w + d, NW)
        k = 2 * b + phase
        if gather:
            src = wide_chunk(r_buf.at[b], w)
            dst = wide_chunk(r_buf.at[b], w)
        else:
            src = wide_chunk(q.at[pl.ds(8 * b, 8)], peer)
            dst = rs_buf.at[b, d - 1]
        return pltpu.make_async_remote_copy(
            src_ref=src, dst_ref=dst, send_sem=wsend.at[k, d], recv_sem=wrecv.at[k, d],
            device_id=wide_dev(peer), device_id_type=MESH,
        )

    def wide_arrival(b, phase, d, gather):
        peer = lax.rem(w + NW - d, NW)
        k = 2 * b + phase
        dst = wide_chunk(r_buf.at[b], peer) if gather else rs_buf.at[b, d - 1]
        return pltpu.make_async_remote_copy(
            src_ref=dst, dst_ref=dst, send_sem=wsend.at[k, d], recv_sem=wrecv.at[k, d],
            device_id=wide_dev(peer), device_id_type=MESH,
        )

    def start_wide(b, gather):
        @pl.loop(1, NW)
        def _(d):
            wide_copy(b, int(gather), d, gather).start()

    def end_wide(b, gather):
        @pl.loop(1, NW)
        def _(d):
            wide_arrival(b, int(gather), d, gather).wait_recv()

    def end_sends(b):
        @pl.loop(1, NW)
        def _(d):
            wide_copy(b, 0, d, False).wait_send()

    def sum_wide(b):
        total = wide_chunk(q.at[pl.ds(8 * b, 8)], w)[...]
        for d in range(NW - 1):
            total = total + rs_buf[b, d]
        wide_chunk(r_buf.at[b], w)[...] = total

    def narrow_copy(b, phase, d):
        peer = lax.rem(n + d, NN)
        k = 2 * b + phase
        mine = pl.ds(pl.multiple_of(n * 8, 8), 8)
        theirs = pl.ds(pl.multiple_of(peer * 8, 8), 8)
        if phase:
            src, dst = wf.at[b, mine], wf.at[b, mine]
        else:
            src, dst = wp.at[b, theirs], nb.at[b, d - 1]
        return pltpu.make_async_remote_copy(
            src_ref=src, dst_ref=dst, send_sem=nsend.at[k, d], recv_sem=nrecv.at[k, d],
            device_id=narrow_dev(peer), device_id_type=MESH,
        )

    def narrow_arrival(b, phase, d):
        peer = lax.rem(n + NN - d, NN)
        k = 2 * b + phase
        theirs = pl.ds(pl.multiple_of(peer * 8, 8), 8)
        dst = wf.at[b, theirs] if phase else nb.at[b, d - 1]
        return pltpu.make_async_remote_copy(
            src_ref=dst, dst_ref=dst, send_sem=nsend.at[k, d], recv_sem=nrecv.at[k, d],
            device_id=narrow_dev(peer), device_id_type=MESH,
        )

    def start_narrow(b, phase):
        @pl.loop(1, NN)
        def _(d):
            narrow_copy(b, phase, d).start()

    def end_narrow(b, phase):
        @pl.loop(1, NN)
        def _(d):
            narrow_arrival(b, phase, d).wait_recv()

    def sum_narrow(b):
        mine = pl.ds(pl.multiple_of(n * 8, 8), 8)
        total = wp[b, mine]
        for d in range(NN - 1):
            total = total + nb[b, d]
        wf[b, mine] = total

    def solve(b):
        for k in range(8):
            at = slice(k * GROUP, (k + 1) * GROUP)
            value = r_buf[b, k]
            hi_part = value.astype(BF16)
            r_hl[0:SAMPLES, at] = hi_part
            r_hl[SAMPLES:, at] = (value - hi_part.astype(F32)).astype(BF16)
        dims = (((1,), (1,)), ((), ()))
        both = lax.dot_general(r_hl[...], inv_hi[b], dims, preferred_element_type=F32)
        low = lax.dot_general(r_hl[0:SAMPLES, :], inv_lo[b], dims, preferred_element_type=F32)
        wp[b] = both[:SAMPLES] + both[SAMPLES:] + low

    def finish_weights(b):
        value = wf[b]
        weights[b] = value
        hi_part = value.astype(BF16)
        w_hl[b, 0:SAMPLES, :] = hi_part
        w_hl[b, SAMPLES:, :] = (value - hi_part.astype(F32)).astype(BF16)

    def apply_pairs(b, lo, hi):
        @pl.loop(lo, hi)
        def _(pair):
            both = jnp.dot(w_hl[b], h_hi[b, pair], preferred_element_type=F32)
            low = jnp.dot(w_hl[b, 0:SAMPLES, :], h_lo[b, pair], preferred_element_type=F32)
            total = both[:SAMPLES] + both[SAMPLES:] + low
            for i in range(2):
                q[2 * pair + i] = q[2 * pair + i] - total[:, i * GROUP : (i + 1) * GROUP]

    def apply_noise(b):
        @pl.when(n == lax.div(w, 2))
        def _():
            for k in range(4):
                at = 8 * b + lax.rem(w, 2) * 4 + k
                q[at] = q[at] - NOISE_VAR * wf[b, :, k * GROUP : (k + 1) * GROUP]

    def rows_copy(d):
        return pltpu.make_async_remote_copy(
            src_ref=rows, dst_ref=rows, send_sem=rsend.at[d], recv_sem=rrecv.at[0],
            device_id=narrow_dev(lax.rem(n + d, NN)), device_id_type=MESH,
        )

    prior_pairs(0, 4)
    pl.semaphore_wait(barrier, NW - 1 + NN - 1)
    start_wide(0, False)
    holder = n == lax.div(w, 2)

    @pl.when(holder)
    def _():
        rows[...] = row_points[...]

        @pl.loop(1, NN)
        def _(d):
            rows_copy(d).start()

    prior_pairs(4, 8)
    end_wide(0, False)
    sum_wide(0)
    start_wide(0, True)

    @pl.when(jnp.logical_not(holder))
    def _():
        pltpu.make_async_remote_copy(
            src_ref=rows, dst_ref=rows, send_sem=rsend.at[0], recv_sem=rrecv.at[0],
            device_id=narrow_dev(lax.rem(n + 1, NN)), device_id_type=MESH,
        ).wait_recv()

    for k in range(8):
        z = (rows[k] - 0.5) * coord_scale
        t = split3(jnp.sum(z * z, axis=0, keepdims=True))
        stack = left_stack(-2.0 * z, rows_of(*t, ones, ones, ones))
        armat[k // 4, (k % 4) * GROUP : (k % 4 + 1) * GROUP, :] = stack.T.astype(BF16)

    inv_copy.wait()

    @pl.loop(0, 2 * ROWS // 64)
    def _(i):
        b = lax.div(i, ROWS // 64)
        at = pl.ds(pl.multiple_of(lax.rem(i, ROWS // 64) * 64, 64), 64)
        value = inv_v[b, at, :]
        hi_part = value.astype(BF16)
        inv_hi[b, at, :] = hi_part
        inv_lo[b, at, :] = (value - hi_part.astype(F32)).astype(BF16)

    kernel_pairs(4, 8)
    prior_pairs(8, 10)
    end_wide(0, True)
    solve(0)
    start_narrow(0, 0)
    prior_pairs(10, 12)
    end_narrow(0, 0)
    sum_narrow(0)
    start_narrow(0, 1)
    prior_pairs(12, 14)
    end_narrow(0, 1)
    finish_weights(0)
    apply_pairs(0, 4, 8)
    start_wide(1, False)
    prior_pairs(14, 16)
    kernel_pairs(0, 4)
    end_wide(1, False)
    sum_wide(1)
    start_wide(1, True)
    kernel_pairs(8, 16)
    end_wide(1, True)
    solve(1)
    start_narrow(1, 0)
    end_sends(0)
    apply_pairs(0, 0, 4)
    apply_noise(0)
    apply_pairs(0, 8, 16)
    end_narrow(1, 0)
    sum_narrow(1)
    start_narrow(1, 1)
    end_narrow(1, 1)
    finish_weights(1)

    end_sends(1)
    apply_pairs(1, 0, 16)
    apply_noise(1)

    for x in range(4):
        for z in range(2):
            for i in range(2):
                own[x, z, i] = q[place[2 * (z * 8 + x * 2 + core) + i]]
                give[x, z, i] = q[place[2 * (z * 8 + x * 2 + 1 - core) + i]]

    core_copy = pltpu.make_async_remote_copy(
        src_ref=give, dst_ref=cbuf, send_sem=fsend.at[0], recv_sem=frecv.at[0],
        device_id=wide_dev(w + 1 - 2 * core), device_id_type=MESH,
    )
    core_copy.start()
    core_copy.wait_recv()
    for x in range(4):
        ubuf[x] = own[x] + cbuf[x]

    def x_copy(d):
        peer = lax.rem(x_here + d, 4)
        return pltpu.make_async_remote_copy(
            src_ref=ubuf.at[peer], dst_ref=xbuf.at[d - 1], send_sem=fsend.at[d], recv_sem=frecv.at[d],
            device_id=wide_dev(z_here * 8 + peer * 2 + core), device_id_type=MESH,
        )

    for d in range(1, 4):
        x_copy(d).start()
    for d in range(1, 4):
        x_copy(d).wait_recv()
    vbuf[...] = ubuf[x_here] + xbuf[0] + xbuf[1] + xbuf[2]
    z_copy = pltpu.make_async_remote_copy(
        src_ref=vbuf.at[1 - z_here], dst_ref=zbuf, send_sem=fsend.at[4], recv_sem=frecv.at[4],
        device_id=wide_dev((1 - z_here) * 8 + x_here * 2 + core), device_id_type=MESH,
    )
    z_copy.start()
    z_copy.wait_recv()
    total = vbuf[z_here] + zbuf[...]
    for i in range(2):
        out[:, i * GROUP : (i + 1) * GROUP] = total[i]

    @pl.loop(1, NW)
    def _(d):
        wide_copy(0, 1, d, True).wait_send()
        wide_copy(1, 1, d, True).wait_send()

    @pl.loop(1, NN)
    def _(d):
        for b in range(2):
            for phase in range(2):
                narrow_copy(b, phase, d).wait_send()

    @pl.when(holder)
    def _():
        @pl.loop(1, NN)
        def _(d):
            rows_copy(d).wait_send()

    core_copy.wait_send()
    for d in range(1, 4):
        x_copy(d).wait_send()
    z_copy.wait_send()


def on_device(points, scales, frequencies, phases, feature_weights, targets, noise, inverses, groups):
    vmem = pl.BlockSpec(memory_space=pltpu.VMEM)
    smem = pl.BlockSpec(memory_space=pltpu.SMEM)
    tile = (SAMPLES, GROUP)
    dma = pltpu.SemaphoreType.DMA
    ordered, row_points, place, mine = pl.pallas_call(
        arrange,
        out_shape=(
            jax.ShapeDtypeStruct((NGROUPS, D, GROUP), F32),
            jax.ShapeDtypeStruct((8, D, GROUP), F32),
            jax.ShapeDtypeStruct((NGROUPS,), jnp.int32),
            jax.ShapeDtypeStruct((2, NGROUPS), F32),
        ),
        in_specs=[smem, vmem],
        out_specs=(vmem, vmem, smem, smem),
        name="arrange",
    )(groups, points)
    return pl.pallas_call(
        body,
        out_shape=(
            jax.ShapeDtypeStruct((SAMPLES, 2 * GROUP), F32),
            jax.ShapeDtypeStruct((2, SAMPLES, ROWS), F32),
        ),
        in_specs=[smem, smem, smem] + [vmem] * 7 + [pl.BlockSpec(memory_space=pl.ANY)],
        out_specs=(vmem, vmem),
        scratch_shapes=[
            pltpu.VMEM((FHERE, KDIM), BF16),
            pltpu.VMEM((NGROUPS, KDIM, GROUP), BF16),
            pltpu.VMEM((NGROUPS, KDIM, GROUP), BF16),
            pltpu.VMEM((2, ROWS, KDIM), BF16),
            pltpu.VMEM((8, D, GROUP), F32),
            pltpu.VMEM((2, *tile), F32),
            pltpu.VMEM((NGROUPS, *tile), F32),
            pltpu.VMEM((2, PAIRS, ROWS, 2 * GROUP), BF16),
            pltpu.VMEM((2, PAIRS, ROWS, 2 * GROUP), BF16),
            pltpu.VMEM((2, ROWS, BCOLS), F32),
            pltpu.VMEM((2, ROWS, BCOLS), BF16),
            pltpu.VMEM((2, ROWS, BCOLS), BF16),
            pltpu.VMEM((2, NW - 1, 32, GROUP), F32),
            pltpu.VMEM((2, 8, *tile), F32),
            pltpu.VMEM((2 * SAMPLES, BCOLS), BF16),
            pltpu.VMEM((2, SAMPLES, ROWS), F32),
            pltpu.VMEM((2, NN - 1, 8, ROWS), F32),
            pltpu.VMEM((2, SAMPLES, ROWS), F32),
            pltpu.VMEM((2, 2 * SAMPLES, ROWS), BF16),
            pltpu.VMEM((4, 2, 2, *tile), F32),
            pltpu.VMEM((4, 2, 2, *tile), F32),
            pltpu.VMEM((4, 2, 2, *tile), F32),
            pltpu.VMEM((4, 2, 2, *tile), F32),
            pltpu.VMEM((3, 2, 2, *tile), F32),
            pltpu.VMEM((2, 2, *tile), F32),
            pltpu.VMEM((2, *tile), F32),
            dma,
            dma((4, NW)),
            dma((4, NW)),
            dma((4, NN)),
            dma((4, NN)),
            dma((NN,)),
            dma((1,)),
            dma((5,)),
            dma((5,)),
        ],
        compiler_params=pltpu.CompilerParams(collective_id=0, has_side_effects=True),
        name="posterior",
    )(
        place, mine, scales, ordered, row_points, frequencies, phases.reshape(1, -1), feature_weights,
        targets.reshape(1, -1), noise, inverses,
    )


def solution(mesh):
    in_specs = (
        P(None, "narrow"),
        P(),
        P(None, "wide"),
        P("wide"),
        P(None, "wide"),
        P(("narrow", "wide")),
        P(None, ("narrow", "wide")),
        P(None, "wide", "narrow"),
        P(),
    )
    out_specs = (P(None, ("narrow", "wide")), P(None, None, "wide"))
    return jax.shard_map(on_device, mesh=mesh, in_specs=in_specs, out_specs=out_specs, check_vma=False)
```

```python
import math

import jax
import jax.numpy as jnp
from jax import lax
from jax.experimental import pallas as pl
from jax.experimental.pallas import tpu as pltpu
from jax.sharding import PartitionSpec as P

F32 = jnp.float32
BF16 = jnp.bfloat16
MESH = pl.DeviceIdType.MESH

D = 8
NW = 16
NN = 8
SAMPLES = 64
GROUP = 128
NGROUPS = 32
PAIRS = 16
KDIM = 64
FHERE = 2048
FCHUNK = 512
ROWS = 512
BCOLS = 1024
NOISE_VAR = 0.1
LN2 = math.log(2.0)
LOG2E = 1.0 / LN2
ROUND = 12582912.0
SIN = (6.283185005, -41.34165573, 81.60100555, -76.54978180, 39.53670502)


def split3(value):
    first = value.astype(BF16).astype(F32)
    rest = value - first
    second = rest.astype(BF16).astype(F32)
    return first, second, rest - second


def rows_of(*rows):
    at = lax.broadcasted_iota(jnp.int32, (8, GROUP), 0)
    result = jnp.zeros((8, GROUP), F32)
    for index, row in enumerate(rows):
        result = jnp.where(at == index, row, result)
    return result


def left_stack(value, extra):
    a, b, c = split3(value)
    return jnp.concatenate([a, a, b, b, a, c, extra, jnp.zeros_like(a)], axis=0)


def right_stack(value, extra):
    a, b, c = split3(value)
    return jnp.concatenate([a, b, a, b, c, a, extra, jnp.zeros_like(a)], axis=0)


def cosine_turns(turns):
    whole = (turns + ROUND) - ROUND
    s = 0.25 - jnp.abs(turns - whole)
    y = s * s
    return s * (SIN[0] + y * (SIN[1] + y * (SIN[2] + y * (SIN[3] + y * SIN[4]))))


def arrange(groups, order, place, mine):
    w = lax.axis_index("wide")
    n = lax.axis_index("narrow")
    for g in range(NGROUPS):
        place[g] = -1
    for g in range(2 * NGROUPS):
        mine[g] = 0.0
    for k in range(16):
        g = lax.rem(groups[k // 8, n * 8 + k % 8], NGROUPS)
        order[k] = g
        place[g] = k
    for k in range(8):
        order[NGROUPS + k] = lax.rem(groups[k // 4, w * 4 + k % 4], NGROUPS)
    count = jnp.int32(16)
    for g in range(NGROUPS):
        at = place[g]
        free = at < 0
        at = jnp.where(free, count, at)
        place[g] = at
        order[at] = g
        count = count + jnp.where(free, 1, 0)
    for i in range(2):
        mine[i * NGROUPS + place[2 * w + i]] = 1.0


def body(
    order, place, mine, scales, points, freq, phases, fw, targets, noise, inverses,
    result,
    amat, bmat, cmat, armat, rows, base, q, h_hi, h_lo, inv_v, inv_hi, inv_lo,
    rs_buf, r_buf, r_hl, wp, nb, wf, w_hl, own, give, cbuf, fbuf, pts,
    inv_sem, wsend, wrecv, nsend, nrecv, rsend, rrecv, csend, crecv, fsend, frecv,
):
    w = lax.axis_index("wide")
    n = lax.axis_index("narrow")
    core = lax.rem(w, 2)
    x_here = lax.rem(lax.div(w, 2), 4)
    z_here = lax.div(w, 8)

    def wide_dev(peer):
        return {"wide": peer}

    def narrow_dev(peer):
        return {"narrow": peer}

    barrier = pltpu.get_barrier_semaphore()

    @pl.loop(1, NW)
    def _(d):
        pl.semaphore_signal(barrier, inc=1, device_id=wide_dev(lax.rem(w + d, NW)), device_id_type=MESH)

    @pl.loop(1, NN)
    def _(d):
        pl.semaphore_signal(barrier, inc=1, device_id=narrow_dev(lax.rem(n + d, NN)), device_id_type=MESH)

    inv_copy = pltpu.make_async_copy(inverses, inv_v, inv_sem)
    inv_copy.start()

    scale_col = jnp.concatenate([jnp.full((1, GROUP), scales[d], F32) for d in range(D)], axis=0)
    coord_scale = scale_col * (math.sqrt(5.0) * LOG2E)
    ones = jnp.ones((1, GROUP), F32)

    @pl.loop(0, FHERE // GROUP)
    def _(k):
        at = pl.ds(pl.multiple_of(k * GROUP, GROUP), GROUP)
        f = freq[:, at] * (0.5 / math.pi)
        ph = split3(phases[:, at] * (0.5 / math.pi))
        amat[at, :] = left_stack(f, rows_of(*ph)).T.astype(BF16)

    @pl.loop(0, NGROUPS)
    def _(g):
        at = pl.ds(pl.multiple_of(g * GROUP, GROUP), GROUP)
        here = points[:, at]
        pts[g] = here
        bmat[g] = right_stack(here, rows_of(ones, ones, ones)).astype(BF16)
        z = (here - 0.5) * coord_scale
        t = split3(jnp.sum(z * z, axis=0, keepdims=True))
        cmat[g] = right_stack(z, rows_of(ones, ones, ones, *t)).astype(BF16)

    for i in range(2):
        at = slice(i * GROUP, (i + 1) * GROUP)
        base[i] = targets[:, at] - noise[:, at]

    def prior_pairs(lo, hi):
        @pl.loop(lo, hi)
        def _(pair):
            rhs = jnp.concatenate([bmat[order[2 * pair]], bmat[order[2 * pair + 1]]], axis=1)
            acc = jnp.zeros((SAMPLES, 2 * GROUP), F32)
            for k in range(FHERE // FCHUNK):
                at = slice(k * FCHUNK, (k + 1) * FCHUNK)
                turns = jnp.dot(amat[at, :], rhs, preferred_element_type=F32)
                features = cosine_turns(turns).astype(BF16)
                acc = acc + jnp.dot(fw[:, at], features, preferred_element_type=F32)
            for i in range(2):
                at = 2 * pair + i
                own_base = mine[at] * base[0] + mine[NGROUPS + at] * base[1]
                q[at] = own_base - acc[:, i * GROUP : (i + 1) * GROUP] * (1.0 / 128.0)

    def kernel_pairs(lo, hi):
        @pl.loop(lo, hi)
        def _(pair):
            rhs = jnp.concatenate([cmat[order[2 * pair]], cmat[order[2 * pair + 1]]], axis=1)
            for b in range(2):
                for k in range(2):
                    at = slice(k * 256, (k + 1) * 256)
                    m = jnp.dot(armat[b, at, :], rhs, preferred_element_type=F32)
                    m = jnp.maximum(m, 1e-12)
                    u = m * lax.rsqrt(m)
                    h = (1.0 + u * LN2 + m * (LN2 * LN2 / 3.0)) * jnp.exp2(-u)
                    hi_part = h.astype(BF16)
                    lo_part = (h - hi_part.astype(F32)).astype(BF16)
                    for i in range(2):
                        half = slice(i * GROUP, (i + 1) * GROUP)
                        h_hi[b, 2 * pair + i, at, :] = hi_part[:, half]
                        h_lo[b, 2 * pair + i, at, :] = lo_part[:, half]

    def wide_chunk(ref, peer):
        return ref.at[lax.div(peer, 2), pl.ds(pl.multiple_of(lax.rem(peer, 2) * 32, 32), 32)]

    def wide_copy(b, phase, d, gather):
        peer = lax.rem(w + d, NW)
        k = 2 * b + phase
        if gather:
            src = wide_chunk(r_buf.at[b], w)
            dst = wide_chunk(r_buf.at[b], w)
        else:
            src = wide_chunk(q.at[pl.ds(8 * b, 8)], peer)
            dst = rs_buf.at[b, d - 1]
        return pltpu.make_async_remote_copy(
            src_ref=src, dst_ref=dst, send_sem=wsend.at[k, d], recv_sem=wrecv.at[k, d],
            device_id=wide_dev(peer), device_id_type=MESH,
        )

    def wide_arrival(b, phase, d, gather):
        peer = lax.rem(w + NW - d, NW)
        k = 2 * b + phase
        dst = wide_chunk(r_buf.at[b], peer) if gather else rs_buf.at[b, d - 1]
        return pltpu.make_async_remote_copy(
            src_ref=dst, dst_ref=dst, send_sem=wsend.at[k, d], recv_sem=wrecv.at[k, d],
            device_id=wide_dev(peer), device_id_type=MESH,
        )

    def start_wide(b, gather):
        @pl.loop(1, NW)
        def _(d):
            wide_copy(b, int(gather), d, gather).start()

    def end_wide(b, gather):
        @pl.loop(1, NW)
        def _(d):
            wide_arrival(b, int(gather), d, gather).wait_recv()

    def end_sends(b):
        @pl.loop(1, NW)
        def _(d):
            wide_copy(b, 0, d, False).wait_send()

    def sum_wide(b):
        total = wide_chunk(q.at[pl.ds(8 * b, 8)], w)[...]
        for d in range(NW - 1):
            total = total + rs_buf[b, d]
        wide_chunk(r_buf.at[b], w)[...] = total

    def narrow_copy(b, phase, d):
        peer = lax.rem(n + d, NN)
        k = 2 * b + phase
        mine = pl.ds(pl.multiple_of(n * 8, 8), 8)
        theirs = pl.ds(pl.multiple_of(peer * 8, 8), 8)
        if phase:
            src, dst = wf.at[b, mine], wf.at[b, mine]
        else:
            src, dst = wp.at[b, theirs], nb.at[b, d - 1]
        return pltpu.make_async_remote_copy(
            src_ref=src, dst_ref=dst, send_sem=nsend.at[k, d], recv_sem=nrecv.at[k, d],
            device_id=narrow_dev(peer), device_id_type=MESH,
        )

    def narrow_arrival(b, phase, d):
        peer = lax.rem(n + NN - d, NN)
        k = 2 * b + phase
        theirs = pl.ds(pl.multiple_of(peer * 8, 8), 8)
        dst = wf.at[b, theirs] if phase else nb.at[b, d - 1]
        return pltpu.make_async_remote_copy(
            src_ref=dst, dst_ref=dst, send_sem=nsend.at[k, d], recv_sem=nrecv.at[k, d],
            device_id=narrow_dev(peer), device_id_type=MESH,
        )

    def start_narrow(b, phase):
        @pl.loop(1, NN)
        def _(d):
            narrow_copy(b, phase, d).start()

    def end_narrow(b, phase):
        @pl.loop(1, NN)
        def _(d):
            narrow_arrival(b, phase, d).wait_recv()

    def sum_narrow(b):
        mine = pl.ds(pl.multiple_of(n * 8, 8), 8)
        total = wp[b, mine]
        for d in range(NN - 1):
            total = total + nb[b, d]
        wf[b, mine] = total

    def solve(b):
        for k in range(8):
            at = slice(k * GROUP, (k + 1) * GROUP)
            value = r_buf[b, k]
            hi_part = value.astype(BF16)
            r_hl[0:SAMPLES, at] = hi_part
            r_hl[SAMPLES:, at] = (value - hi_part.astype(F32)).astype(BF16)
        dims = (((1,), (1,)), ((), ()))
        both = lax.dot_general(r_hl[...], inv_hi[b], dims, preferred_element_type=F32)
        low = lax.dot_general(r_hl[0:SAMPLES, :], inv_lo[b], dims, preferred_element_type=F32)
        wp[b] = both[:SAMPLES] + both[SAMPLES:] + low

    def finish_weights(b):
        value = wf[b]
        result[:, 2 * GROUP + b * ROWS : 2 * GROUP + (b + 1) * ROWS] = value
        hi_part = value.astype(BF16)
        w_hl[b, 0:SAMPLES, :] = hi_part
        w_hl[b, SAMPLES:, :] = (value - hi_part.astype(F32)).astype(BF16)

    def change(b, p0, p1):
        hi_tile = jnp.concatenate([h_hi[b, p0], h_hi[b, p1]], axis=1)
        lo_tile = jnp.concatenate([h_lo[b, p0], h_lo[b, p1]], axis=1)
        both = jnp.dot(w_hl[b], hi_tile, preferred_element_type=F32)
        low = jnp.dot(w_hl[b, 0:SAMPLES, :], lo_tile, preferred_element_type=F32)
        return both[:SAMPLES] + both[SAMPLES:] + low

    def apply_pairs(b, lo, hi):
        @pl.loop(lo, hi)
        def _(pair):
            total = change(b, 2 * pair, 2 * pair + 1)
            for i in range(2):
                q[2 * pair + i] = q[2 * pair + i] - total[:, i * GROUP : (i + 1) * GROUP]

    def apply_noise(b):
        @pl.when(n == lax.div(w, 2))
        def _():
            for k in range(4):
                at = 8 * b + lax.rem(w, 2) * 4 + k
                q[at] = q[at] - NOISE_VAR * wf[b, :, k * GROUP : (k + 1) * GROUP]

    def rows_copy(d):
        return pltpu.make_async_remote_copy(
            src_ref=rows, dst_ref=rows, send_sem=rsend.at[d], recv_sem=rrecv.at[0],
            device_id=narrow_dev(lax.rem(n + d, NN)), device_id_type=MESH,
        )

    prior_pairs(0, 4)
    pl.semaphore_wait(barrier, NW - 1 + NN - 1)
    start_wide(0, False)
    holder = n == lax.div(w, 2)

    @pl.when(holder)
    def _():
        for k in range(8):
            rows[k] = pts[order[NGROUPS + k]]

        @pl.loop(1, NN)
        def _(d):
            rows_copy(d).start()

    prior_pairs(4, 8)
    end_wide(0, False)
    sum_wide(0)
    start_wide(0, True)

    @pl.when(jnp.logical_not(holder))
    def _():
        pltpu.make_async_remote_copy(
            src_ref=rows, dst_ref=rows, send_sem=rsend.at[0], recv_sem=rrecv.at[0],
            device_id=narrow_dev(lax.rem(n + 1, NN)), device_id_type=MESH,
        ).wait_recv()

    for k in range(8):
        z = (rows[k] - 0.5) * coord_scale
        t = split3(jnp.sum(z * z, axis=0, keepdims=True))
        stack = left_stack(-2.0 * z, rows_of(*t, ones, ones, ones))
        armat[k // 4, (k % 4) * GROUP : (k % 4 + 1) * GROUP, :] = stack.T.astype(BF16)

    inv_copy.wait()

    @pl.loop(0, 2 * ROWS // 64)
    def _(i):
        b = lax.div(i, ROWS // 64)
        at = pl.ds(pl.multiple_of(lax.rem(i, ROWS // 64) * 64, 64), 64)
        value = inv_v[b, at, :]
        hi_part = value.astype(BF16)
        inv_hi[b, at, :] = hi_part
        inv_lo[b, at, :] = (value - hi_part.astype(F32)).astype(BF16)

    kernel_pairs(4, 8)
    prior_pairs(8, 10)
    end_wide(0, True)
    solve(0)
    start_narrow(0, 0)
    prior_pairs(10, 12)
    end_narrow(0, 0)
    sum_narrow(0)
    start_narrow(0, 1)
    prior_pairs(12, 14)
    end_narrow(0, 1)
    finish_weights(0)
    apply_pairs(0, 4, 8)
    start_wide(1, False)
    prior_pairs(14, 16)
    kernel_pairs(0, 4)
    end_wide(1, False)
    sum_wide(1)
    start_wide(1, True)
    kernel_pairs(8, 16)
    end_wide(1, True)
    solve(1)
    start_narrow(1, 0)
    end_sends(0)
    apply_pairs(0, 0, 4)
    apply_noise(0)
    apply_pairs(0, 8, 16)
    end_narrow(1, 0)
    sum_narrow(1)
    start_narrow(1, 1)
    end_narrow(1, 1)
    finish_weights(1)

    end_sends(1)
    apply_noise(1)

    def chip(rel):
        return lax.rem(z_here + lax.div(rel, 4), 2) * 8 + lax.rem(x_here + lax.rem(rel, 4), 4) * 2

    def final_piece(dest):
        p0, p1 = place[2 * dest], place[2 * dest + 1]
        total = change(1, p0, p1)
        return q[p0] - total[:, :GROUP], q[p1] - total[:, GROUP:]

    def core_copy(rel):
        return pltpu.make_async_remote_copy(
            src_ref=give.at[rel], dst_ref=cbuf.at[rel], send_sem=csend.at[rel], recv_sem=crecv.at[rel],
            device_id=wide_dev(w + 1 - 2 * core), device_id_type=MESH,
        )

    def chip_copy(rel):
        return pltpu.make_async_remote_copy(
            src_ref=own.at[rel], dst_ref=fbuf.at[rel - 1], send_sem=fsend.at[rel], recv_sem=frecv.at[rel],
            device_id=wide_dev(chip(rel) + core), device_id_type=MESH,
        )

    @pl.loop(0, 8)
    def _(j):
        rel = 7 - j
        piece = final_piece(chip(rel) + 1 - core)
        for i in range(2):
            give[rel, i] = piece[i]
        core_copy(rel).start()

    @pl.loop(0, 7)
    def _(j):
        rel = 7 - j
        piece = final_piece(chip(rel) + core)
        core_copy(rel).wait_recv()
        for i in range(2):
            own[rel, i] = piece[i] + cbuf[rel, i]
        chip_copy(rel).start()

    piece = final_piece(w)
    core_copy(0).wait_recv()
    total = [piece[i] + cbuf[0, i] for i in range(2)]
    for rel in range(7, 0, -1):
        chip_copy(rel).wait_recv()
        total = [total[i] + fbuf[rel - 1, i] for i in range(2)]
    for i in range(2):
        result[:, i * GROUP : (i + 1) * GROUP] = total[i]

    @pl.loop(1, NW)
    def _(d):
        wide_copy(0, 1, d, True).wait_send()
        wide_copy(1, 1, d, True).wait_send()

    @pl.loop(1, NN)
    def _(d):
        for b in range(2):
            for phase in range(2):
                narrow_copy(b, phase, d).wait_send()

    @pl.when(holder)
    def _():
        @pl.loop(1, NN)
        def _(d):
            rows_copy(d).wait_send()

    @pl.loop(0, 8)
    def _(rel):
        core_copy(rel).wait_send()

    @pl.loop(1, 8)
    def _(rel):
        chip_copy(rel).wait_send()


def unpack(result, residual, weights):
    residual[...] = result[:, : 2 * GROUP]
    for b in range(2):
        weights[b] = result[:, 2 * GROUP + b * ROWS : 2 * GROUP + (b + 1) * ROWS]


def on_device(points, scales, frequencies, phases, feature_weights, targets, noise, inverses, groups):
    vmem = pl.BlockSpec(memory_space=pltpu.VMEM)
    smem = pl.BlockSpec(memory_space=pltpu.SMEM)
    tile = (SAMPLES, GROUP)
    dma = pltpu.SemaphoreType.DMA
    order, place, mine = pl.pallas_call(
        arrange,
        out_shape=(
            jax.ShapeDtypeStruct((NGROUPS + 8,), jnp.int32),
            jax.ShapeDtypeStruct((NGROUPS,), jnp.int32),
            jax.ShapeDtypeStruct((2 * NGROUPS,), F32),
        ),
        in_specs=[smem],
        out_specs=(smem, smem, smem),
        name="arrange",
    )(groups)
    result = pl.pallas_call(
        body,
        out_shape=jax.ShapeDtypeStruct((SAMPLES, 2 * GROUP + 2 * ROWS), F32),
        in_specs=[smem] * 4 + [vmem] * 6 + [pl.BlockSpec(memory_space=pl.ANY)],
        out_specs=vmem,
        scratch_shapes=[
            pltpu.VMEM((FHERE, KDIM), BF16),
            pltpu.VMEM((NGROUPS, KDIM, GROUP), BF16),
            pltpu.VMEM((NGROUPS, KDIM, GROUP), BF16),
            pltpu.VMEM((2, ROWS, KDIM), BF16),
            pltpu.VMEM((8, D, GROUP), F32),
            pltpu.VMEM((2, *tile), F32),
            pltpu.VMEM((NGROUPS, *tile), F32),
            pltpu.VMEM((2, NGROUPS, ROWS, GROUP), BF16),
            pltpu.VMEM((2, NGROUPS, ROWS, GROUP), BF16),
            pltpu.VMEM((2, ROWS, BCOLS), F32),
            pltpu.VMEM((2, ROWS, BCOLS), BF16),
            pltpu.VMEM((2, ROWS, BCOLS), BF16),
            pltpu.VMEM((2, NW - 1, 32, GROUP), F32),
            pltpu.VMEM((2, 8, *tile), F32),
            pltpu.VMEM((2 * SAMPLES, BCOLS), BF16),
            pltpu.VMEM((2, SAMPLES, ROWS), F32),
            pltpu.VMEM((2, NN - 1, 8, ROWS), F32),
            pltpu.VMEM((2, SAMPLES, ROWS), F32),
            pltpu.VMEM((2, 2 * SAMPLES, ROWS), BF16),
            pltpu.VMEM((8, 2, *tile), F32),
            pltpu.VMEM((8, 2, *tile), F32),
            pltpu.VMEM((8, 2, *tile), F32),
            pltpu.VMEM((7, 2, *tile), F32),
            pltpu.VMEM((NGROUPS, D, GROUP), F32),
            dma,
            dma((4, NW)),
            dma((4, NW)),
            dma((4, NN)),
            dma((4, NN)),
            dma((NN,)),
            dma((1,)),
            dma((8,)),
            dma((8,)),
            dma((8,)),
            dma((8,)),
        ],
        compiler_params=pltpu.CompilerParams(collective_id=0, has_side_effects=True),
        name="posterior",
    )(
        order, place, mine, scales, points, frequencies, phases.reshape(1, -1), feature_weights,
        targets.reshape(1, -1), noise, inverses,
    )
    return pl.pallas_call(
        unpack,
        out_shape=(
            jax.ShapeDtypeStruct((SAMPLES, 2 * GROUP), F32),
            jax.ShapeDtypeStruct((2, SAMPLES, ROWS), F32),
        ),
        in_specs=[vmem],
        out_specs=(vmem, vmem),
        name="unpack",
    )(result)


def solution(mesh):
    in_specs = (
        P(None, "narrow"),
        P(),
        P(None, "wide"),
        P("wide"),
        P(None, "wide"),
        P(("narrow", "wide")),
        P(None, ("narrow", "wide")),
        P(None, "wide", "narrow"),
        P(),
    )
    out_specs = (P(None, ("narrow", "wide")), P(None, None, "wide"))
    return jax.shard_map(on_device, mesh=mesh, in_specs=in_specs, out_specs=out_specs, check_vma=False)
```

```python
import math

import jax
import jax.numpy as jnp
from jax import lax
from jax.experimental import pallas as pl
from jax.experimental.pallas import tpu as pltpu
from jax.sharding import PartitionSpec as P

F32 = jnp.float32
BF16 = jnp.bfloat16
MESH = pl.DeviceIdType.MESH

D = 8
NW = 16
NN = 8
SAMPLES = 64
GROUP = 128
NGROUPS = 32
PAIRS = 16
KDIM = 64
FHERE = 2048
FCHUNK = 512
ROWS = 512
BCOLS = 1024
NOISE_VAR = 0.1
LN2 = math.log(2.0)
LOG2E = 1.0 / LN2
ROUND = 12582912.0
WIDE_ORDER = (12, 13, 10, 11, 14, 15, 4, 5, 8, 9, 2, 3, 6, 7, 1)
NARROW_ORDER = (6, 5, 7, 2, 1, 3, 4)
SIN = (6.283185005, -41.34165573, 81.60100555, -76.54978180, 39.53670502)


def split3(value):
    first = value.astype(BF16).astype(F32)
    rest = value - first
    second = rest.astype(BF16).astype(F32)
    return first, second, rest - second


def rows_of(*rows):
    at = lax.broadcasted_iota(jnp.int32, (8, GROUP), 0)
    result = jnp.zeros((8, GROUP), F32)
    for index, row in enumerate(rows):
        result = jnp.where(at == index, row, result)
    return result


def left_stack(value, extra):
    a, b, c = split3(value)
    return jnp.concatenate([a, a, b, b, a, c, extra, jnp.zeros_like(a)], axis=0)


def right_stack(value, extra):
    a, b, c = split3(value)
    return jnp.concatenate([a, b, a, b, c, a, extra, jnp.zeros_like(a)], axis=0)


def cosine_turns(turns):
    whole = (turns + ROUND) - ROUND
    s = 0.25 - jnp.abs(turns - whole)
    y = s * s
    return s * (SIN[0] + y * (SIN[1] + y * (SIN[2] + y * (SIN[3] + y * SIN[4]))))


def arrange(groups, order, place, mine):
    w = lax.axis_index("wide")
    n = lax.axis_index("narrow")
    for g in range(NGROUPS):
        place[g] = -1
    for g in range(2 * NGROUPS):
        mine[g] = 0.0
    for k in range(16):
        g = lax.rem(groups[k // 8, n * 8 + k % 8], NGROUPS)
        order[k] = g
        place[g] = k
    for k in range(8):
        order[NGROUPS + k] = lax.rem(groups[k // 4, w * 4 + k % 4], NGROUPS)
    count = jnp.int32(16)
    for g in range(NGROUPS):
        at = place[g]
        free = at < 0
        at = jnp.where(free, count, at)
        place[g] = at
        order[at] = g
        count = count + jnp.where(free, 1, 0)
    for i in range(2):
        mine[i * NGROUPS + place[2 * w + i]] = 1.0


def body(
    order, place, mine, scales, points, freq, phases, fw, targets, noise, inverses,
    result,
    amat, bmat, cmat, armat, rows, base, q, h_hi, h_lo, inv_v, inv_hi, inv_lo,
    rs_buf, r_buf, r_hl, wp, nb, wf, w_hl, own, give, cbuf, fbuf, pts,
    inv_sem, wsend, wrecv, nsend, nrecv, rsend, rrecv, csend, crecv, fsend, frecv,
):
    w = lax.axis_index("wide")
    n = lax.axis_index("narrow")
    core = lax.rem(w, 2)
    x_here = lax.rem(lax.div(w, 2), 4)
    z_here = lax.div(w, 8)

    def wide_dev(peer):
        return {"wide": peer}

    def narrow_dev(peer):
        return {"narrow": peer}

    barrier = pltpu.get_barrier_semaphore()

    @pl.loop(1, NW)
    def _(d):
        pl.semaphore_signal(barrier, inc=1, device_id=wide_dev(lax.rem(w + d, NW)), device_id_type=MESH)

    @pl.loop(1, NN)
    def _(d):
        pl.semaphore_signal(barrier, inc=1, device_id=narrow_dev(lax.rem(n + d, NN)), device_id_type=MESH)

    inv_copy = pltpu.make_async_copy(inverses, inv_v, inv_sem)
    inv_copy.start()

    scale_col = jnp.concatenate([jnp.full((1, GROUP), scales[d], F32) for d in range(D)], axis=0)
    coord_scale = scale_col * (math.sqrt(5.0) * LOG2E)
    ones = jnp.ones((1, GROUP), F32)

    for k in range(FHERE // GROUP):
        at = slice(k * GROUP, (k + 1) * GROUP)
        f = freq[:, at] * (0.5 / math.pi)
        ph = split3(phases[:, at] * (0.5 / math.pi))
        amat[at, :] = left_stack(f, rows_of(*ph)).T.astype(BF16)

    for g in range(NGROUPS):
        pts[g] = points[:, g * GROUP : (g + 1) * GROUP]

    def point_operands(lo, hi):
        @pl.loop(lo, hi, unroll=4)
        def _(k):
            bmat[k] = right_stack(pts[order[k]], rows_of(ones, ones, ones)).astype(BF16)

    def kernel_operands():
        @pl.loop(0, NGROUPS, unroll=4)
        def _(k):
            z = (pts[order[k]] - 0.5) * coord_scale
            t = split3(jnp.sum(z * z, axis=0, keepdims=True))
            cmat[k] = right_stack(z, rows_of(ones, ones, ones, *t)).astype(BF16)

    point_operands(0, 8)
    for i in range(2):
        at = slice(i * GROUP, (i + 1) * GROUP)
        base[i] = targets[:, at] - noise[:, at]

    def prior_pairs(lo, hi):
        @pl.loop(lo, hi)
        def _(pair):
            rhs = jnp.concatenate([bmat[2 * pair], bmat[2 * pair + 1]], axis=1)
            acc = jnp.zeros((SAMPLES, 2 * GROUP), F32)
            for k in range(FHERE // FCHUNK):
                at = slice(k * FCHUNK, (k + 1) * FCHUNK)
                turns = jnp.dot(amat[at, :], rhs, preferred_element_type=F32)
                features = cosine_turns(turns).astype(BF16)
                acc = acc + jnp.dot(fw[:, at], features, preferred_element_type=F32)
            for i in range(2):
                at = 2 * pair + i
                own_base = mine[at] * base[0] + mine[NGROUPS + at] * base[1]
                q[at] = own_base - acc[:, i * GROUP : (i + 1) * GROUP] * (1.0 / 128.0)

    def kernel_pairs(lo, hi):
        @pl.loop(lo, hi)
        def _(pair):
            rhs = jnp.concatenate([cmat[2 * pair], cmat[2 * pair + 1]], axis=1)
            for b in range(2):
                for k in range(2):
                    at = slice(k * 256, (k + 1) * 256)
                    m = jnp.dot(armat[b, at, :], rhs, preferred_element_type=F32)
                    m = jnp.maximum(m, 1e-12)
                    u = m * lax.rsqrt(m)
                    h = (1.0 + u * LN2 + m * (LN2 * LN2 / 3.0)) * jnp.exp2(-u)
                    hi_part = h.astype(BF16)
                    lo_part = (h - hi_part.astype(F32)).astype(BF16)
                    for i in range(2):
                        half = slice(i * GROUP, (i + 1) * GROUP)
                        h_hi[b, 2 * pair + i, at, :] = hi_part[:, half]
                        h_lo[b, 2 * pair + i, at, :] = lo_part[:, half]

    def wide_chunk(ref, peer):
        return ref.at[lax.div(peer, 2), pl.ds(pl.multiple_of(lax.rem(peer, 2) * 32, 32), 32)]

    def wide_peer(rel, sign):
        z, x, c = rel // 8, rel // 2 % 4, rel % 2
        return (
            lax.rem(z_here + z, 2) * 8 + lax.rem(x_here + (x if sign > 0 else 4 - x), 4) * 2 + lax.rem(core + c, 2)
        )

    def narrow_peer(rel, sign):
        z, y = rel // 4, rel % 4
        return lax.rem(lax.div(n, 4) + z, 2) * 4 + lax.rem(lax.rem(n, 4) + (y if sign > 0 else 4 - y), 4)

    def wide_copy(b, gather, rel):
        peer = wide_peer(rel, 1)
        k = 2 * b + gather
        if gather:
            src = wide_chunk(r_buf.at[b], w)
            dst = wide_chunk(r_buf.at[b], w)
        else:
            src = wide_chunk(q.at[pl.ds(8 * b, 8)], peer)
            dst = rs_buf.at[b, rel - 1]
        return pltpu.make_async_remote_copy(
            src_ref=src, dst_ref=dst, send_sem=wsend.at[k, rel], recv_sem=wrecv.at[k, rel],
            device_id=wide_dev(peer), device_id_type=MESH,
        )

    def wide_arrival(b, gather, rel):
        peer = wide_peer(rel, -1)
        k = 2 * b + gather
        dst = wide_chunk(r_buf.at[b], peer) if gather else rs_buf.at[b, rel - 1]
        return pltpu.make_async_remote_copy(
            src_ref=dst, dst_ref=dst, send_sem=wsend.at[k, rel], recv_sem=wrecv.at[k, rel],
            device_id=wide_dev(peer), device_id_type=MESH,
        )

    def start_wide(b, gather):
        for rel in WIDE_ORDER:
            wide_copy(b, gather, rel).start()

    def end_wide(b, gather):
        for rel in reversed(WIDE_ORDER):
            wide_arrival(b, gather, rel).wait_recv()

    def end_sends(b):
        for rel in WIDE_ORDER:
            wide_copy(b, 0, rel).wait_send()

    def sum_wide(b):
        total = wide_chunk(q.at[pl.ds(8 * b, 8)], w)[...]
        for d in range(NW - 1):
            total = total + rs_buf[b, d]
        wide_chunk(r_buf.at[b], w)[...] = total

    def narrow_copy(b, phase, rel):
        peer = narrow_peer(rel, 1)
        k = 2 * b + phase
        mine = pl.ds(pl.multiple_of(n * 8, 8), 8)
        theirs = pl.ds(pl.multiple_of(peer * 8, 8), 8)
        if phase:
            src, dst = wf.at[b, mine], wf.at[b, mine]
        else:
            src, dst = wp.at[b, theirs], nb.at[b, rel - 1]
        return pltpu.make_async_remote_copy(
            src_ref=src, dst_ref=dst, send_sem=nsend.at[k, rel], recv_sem=nrecv.at[k, rel],
            device_id=narrow_dev(peer), device_id_type=MESH,
        )

    def narrow_arrival(b, phase, rel):
        peer = narrow_peer(rel, -1)
        k = 2 * b + phase
        theirs = pl.ds(pl.multiple_of(peer * 8, 8), 8)
        dst = wf.at[b, theirs] if phase else nb.at[b, rel - 1]
        return pltpu.make_async_remote_copy(
            src_ref=dst, dst_ref=dst, send_sem=nsend.at[k, rel], recv_sem=nrecv.at[k, rel],
            device_id=narrow_dev(peer), device_id_type=MESH,
        )

    def start_narrow(b, phase):
        for rel in NARROW_ORDER:
            narrow_copy(b, phase, rel).start()

    def end_narrow(b, phase):
        for rel in reversed(NARROW_ORDER):
            narrow_arrival(b, phase, rel).wait_recv()

    def sum_narrow(b):
        mine = pl.ds(pl.multiple_of(n * 8, 8), 8)
        total = wp[b, mine]
        for d in range(NN - 1):
            total = total + nb[b, d]
        wf[b, mine] = total

    def solve(b):
        for k in range(8):
            at = slice(k * GROUP, (k + 1) * GROUP)
            value = r_buf[b, k]
            hi_part = value.astype(BF16)
            r_hl[0:SAMPLES, at] = hi_part
            r_hl[SAMPLES:, at] = (value - hi_part.astype(F32)).astype(BF16)
        dims = (((1,), (1,)), ((), ()))
        both = lax.dot_general(r_hl[...], inv_hi[b], dims, preferred_element_type=F32)
        low = lax.dot_general(r_hl[0:SAMPLES, :], inv_lo[b], dims, preferred_element_type=F32)
        wp[b] = both[:SAMPLES] + both[SAMPLES:] + low

    def finish_weights(b):
        value = wf[b]
        result[:, 2 * GROUP + b * ROWS : 2 * GROUP + (b + 1) * ROWS] = value
        hi_part = value.astype(BF16)
        w_hl[b, 0:SAMPLES, :] = hi_part
        w_hl[b, SAMPLES:, :] = (value - hi_part.astype(F32)).astype(BF16)

    def change(b, p0, p1):
        hi_tile = jnp.concatenate([h_hi[b, p0], h_hi[b, p1]], axis=1)
        lo_tile = jnp.concatenate([h_lo[b, p0], h_lo[b, p1]], axis=1)
        both = jnp.dot(w_hl[b], hi_tile, preferred_element_type=F32)
        low = jnp.dot(w_hl[b, 0:SAMPLES, :], lo_tile, preferred_element_type=F32)
        return both[:SAMPLES] + both[SAMPLES:] + low

    def apply_pairs(b, lo, hi):
        @pl.loop(lo, hi)
        def _(pair):
            total = change(b, 2 * pair, 2 * pair + 1)
            for i in range(2):
                q[2 * pair + i] = q[2 * pair + i] - total[:, i * GROUP : (i + 1) * GROUP]

    def apply_noise(b):
        @pl.when(n == lax.div(w, 2))
        def _():
            for k in range(4):
                at = 8 * b + lax.rem(w, 2) * 4 + k
                q[at] = q[at] - NOISE_VAR * wf[b, :, k * GROUP : (k + 1) * GROUP]

    def rows_copy(d):
        return pltpu.make_async_remote_copy(
            src_ref=rows, dst_ref=rows, send_sem=rsend.at[d], recv_sem=rrecv.at[0],
            device_id=narrow_dev(lax.rem(n + d, NN)), device_id_type=MESH,
        )

    prior_pairs(0, 4)
    pl.semaphore_wait(barrier, NW - 1 + NN - 1)
    start_wide(0, 0)
    holder = n == lax.div(w, 2)

    @pl.when(holder)
    def _():
        for k in range(8):
            rows[k] = pts[order[NGROUPS + k]]

        @pl.loop(1, NN)
        def _(d):
            rows_copy(d).start()

    point_operands(8, 16)
    prior_pairs(4, 8)
    end_wide(0, 0)
    sum_wide(0)
    start_wide(0, 1)

    @pl.when(jnp.logical_not(holder))
    def _():
        pltpu.make_async_remote_copy(
            src_ref=rows, dst_ref=rows, send_sem=rsend.at[0], recv_sem=rrecv.at[0],
            device_id=narrow_dev(lax.rem(n + 1, NN)), device_id_type=MESH,
        ).wait_recv()

    point_operands(16, NGROUPS)
    kernel_operands()
    for k in range(8):
        z = (rows[k] - 0.5) * coord_scale
        t = split3(jnp.sum(z * z, axis=0, keepdims=True))
        stack = left_stack(-2.0 * z, rows_of(*t, ones, ones, ones))
        armat[k // 4, (k % 4) * GROUP : (k % 4 + 1) * GROUP, :] = stack.T.astype(BF16)

    inv_copy.wait()

    @pl.loop(0, 2 * ROWS // 64)
    def _(i):
        b = lax.div(i, ROWS // 64)
        at = pl.ds(pl.multiple_of(lax.rem(i, ROWS // 64) * 64, 64), 64)
        value = inv_v[b, at, :]
        hi_part = value.astype(BF16)
        inv_hi[b, at, :] = hi_part
        inv_lo[b, at, :] = (value - hi_part.astype(F32)).astype(BF16)

    kernel_pairs(4, 6)
    end_wide(0, 1)
    solve(0)
    start_narrow(0, 0)
    kernel_pairs(6, 8)
    prior_pairs(8, 10)
    end_narrow(0, 0)
    sum_narrow(0)
    start_narrow(0, 1)
    prior_pairs(10, 13)
    end_narrow(0, 1)
    finish_weights(0)
    apply_pairs(0, 4, 8)
    start_wide(1, 0)
    prior_pairs(13, 16)
    kernel_pairs(0, 2)
    end_wide(1, 0)
    sum_wide(1)
    start_wide(1, 1)
    kernel_pairs(2, 4)
    kernel_pairs(8, 13)
    end_wide(1, 1)
    solve(1)
    start_narrow(1, 0)
    kernel_pairs(13, 16)
    end_sends(0)
    apply_pairs(0, 0, 4)
    apply_noise(0)
    end_narrow(1, 0)
    sum_narrow(1)
    start_narrow(1, 1)
    apply_pairs(0, 8, 16)
    end_sends(1)
    end_narrow(1, 1)
    finish_weights(1)

    apply_noise(1)

    def chip(rel):
        return lax.rem(z_here + lax.div(rel, 4), 2) * 8 + lax.rem(x_here + lax.rem(rel, 4), 4) * 2

    def final_piece(dest):
        p0, p1 = place[2 * dest], place[2 * dest + 1]
        total = change(1, p0, p1)
        return q[p0] - total[:, :GROUP], q[p1] - total[:, GROUP:]

    def core_copy(rel):
        return pltpu.make_async_remote_copy(
            src_ref=give.at[rel], dst_ref=cbuf.at[rel], send_sem=csend.at[rel], recv_sem=crecv.at[rel],
            device_id=wide_dev(w + 1 - 2 * core), device_id_type=MESH,
        )

    def chip_copy(rel):
        return pltpu.make_async_remote_copy(
            src_ref=own.at[rel], dst_ref=fbuf.at[rel - 1], send_sem=fsend.at[rel], recv_sem=frecv.at[rel],
            device_id=wide_dev(chip(rel) + core), device_id_type=MESH,
        )

    def for_other(rel):
        piece = final_piece(chip(rel) + 1 - core)
        for i in range(2):
            give[rel, i] = piece[i]
        core_copy(rel).start()

    for_other(7)

    @pl.loop(0, 7)
    def _(j):
        for_other(6 - j)
        rel = 7 - j
        piece = final_piece(chip(rel) + core)
        core_copy(rel).wait_recv()
        for i in range(2):
            own[rel, i] = piece[i] + cbuf[rel, i]
        chip_copy(rel).start()

    piece = final_piece(w)
    core_copy(0).wait_recv()
    total = [piece[i] + cbuf[0, i] for i in range(2)]
    for rel in range(7, 0, -1):
        chip_copy(rel).wait_recv()
        total = [total[i] + fbuf[rel - 1, i] for i in range(2)]
    for i in range(2):
        result[:, i * GROUP : (i + 1) * GROUP] = total[i]

    for b in range(2):
        for rel in WIDE_ORDER:
            wide_copy(b, 1, rel).wait_send()
        for rel in NARROW_ORDER:
            for phase in range(2):
                narrow_copy(b, phase, rel).wait_send()

    @pl.when(holder)
    def _():
        @pl.loop(1, NN)
        def _(d):
            rows_copy(d).wait_send()

    @pl.loop(0, 8)
    def _(rel):
        core_copy(rel).wait_send()

    @pl.loop(1, 8)
    def _(rel):
        chip_copy(rel).wait_send()


def unpack(result, residual, weights):
    residual[...] = result[:, : 2 * GROUP]
    for b in range(2):
        weights[b] = result[:, 2 * GROUP + b * ROWS : 2 * GROUP + (b + 1) * ROWS]


def on_device(points, scales, frequencies, phases, feature_weights, targets, noise, inverses, groups):
    vmem = pl.BlockSpec(memory_space=pltpu.VMEM)
    smem = pl.BlockSpec(memory_space=pltpu.SMEM)
    tile = (SAMPLES, GROUP)
    dma = pltpu.SemaphoreType.DMA
    order, place, mine = pl.pallas_call(
        arrange,
        out_shape=(
            jax.ShapeDtypeStruct((NGROUPS + 8,), jnp.int32),
            jax.ShapeDtypeStruct((NGROUPS,), jnp.int32),
            jax.ShapeDtypeStruct((2 * NGROUPS,), F32),
        ),
        in_specs=[smem],
        out_specs=(smem, smem, smem),
        name="arrange",
    )(groups)
    result = pl.pallas_call(
        body,
        out_shape=jax.ShapeDtypeStruct((SAMPLES, 2 * GROUP + 2 * ROWS), F32),
        in_specs=[smem] * 4 + [vmem] * 6 + [pl.BlockSpec(memory_space=pl.ANY)],
        out_specs=vmem,
        scratch_shapes=[
            pltpu.VMEM((FHERE, KDIM), BF16),
            pltpu.VMEM((NGROUPS, KDIM, GROUP), BF16),
            pltpu.VMEM((NGROUPS, KDIM, GROUP), BF16),
            pltpu.VMEM((2, ROWS, KDIM), BF16),
            pltpu.VMEM((8, D, GROUP), F32),
            pltpu.VMEM((2, *tile), F32),
            pltpu.VMEM((NGROUPS, *tile), F32),
            pltpu.VMEM((2, NGROUPS, ROWS, GROUP), BF16),
            pltpu.VMEM((2, NGROUPS, ROWS, GROUP), BF16),
            pltpu.VMEM((2, ROWS, BCOLS), F32),
            pltpu.VMEM((2, ROWS, BCOLS), BF16),
            pltpu.VMEM((2, ROWS, BCOLS), BF16),
            pltpu.VMEM((2, NW - 1, 32, GROUP), F32),
            pltpu.VMEM((2, 8, *tile), F32),
            pltpu.VMEM((2 * SAMPLES, BCOLS), BF16),
            pltpu.VMEM((2, SAMPLES, ROWS), F32),
            pltpu.VMEM((2, NN - 1, 8, ROWS), F32),
            pltpu.VMEM((2, SAMPLES, ROWS), F32),
            pltpu.VMEM((2, 2 * SAMPLES, ROWS), BF16),
            pltpu.VMEM((8, 2, *tile), F32),
            pltpu.VMEM((8, 2, *tile), F32),
            pltpu.VMEM((8, 2, *tile), F32),
            pltpu.VMEM((7, 2, *tile), F32),
            pltpu.VMEM((NGROUPS, D, GROUP), F32),
            dma,
            dma((4, NW)),
            dma((4, NW)),
            dma((4, NN)),
            dma((4, NN)),
            dma((NN,)),
            dma((1,)),
            dma((8,)),
            dma((8,)),
            dma((8,)),
            dma((8,)),
        ],
        compiler_params=pltpu.CompilerParams(collective_id=0, has_side_effects=True),
        name="posterior",
    )(
        order, place, mine, scales, points, frequencies, phases.reshape(1, -1), feature_weights,
        targets.reshape(1, -1), noise, inverses,
    )
    return pl.pallas_call(
        unpack,
        out_shape=(
            jax.ShapeDtypeStruct((SAMPLES, 2 * GROUP), F32),
            jax.ShapeDtypeStruct((2, SAMPLES, ROWS), F32),
        ),
        in_specs=[vmem],
        out_specs=(vmem, vmem),
        name="unpack",
    )(result)


def solution(mesh):
    in_specs = (
        P(None, "narrow"),
        P(),
        P(None, "wide"),
        P("wide"),
        P(None, "wide"),
        P(("narrow", "wide")),
        P(None, ("narrow", "wide")),
        P(None, "wide", "narrow"),
        P(),
    )
    out_specs = (P(None, ("narrow", "wide")), P(None, None, "wide"))
    return jax.shard_map(on_device, mesh=mesh, in_specs=in_specs, out_specs=out_specs, check_vma=False)
```
